32 devices in a mesh: dp: 4 (over z), row: 4 (over y, x), col: 2 (over core).
Axes of the slice: x: 2, y: 2, z: 4, core: 2. Of those that a mesh axis runs over, the one named last changes fastest.
Arguments:
- tokens: bfloat16 [16384, 1024], P(('dp', 'col'), 'row'), may hold values from -6 to 6
- first_norm_gain: float32 [1024], P('row'), may hold values from 0.4 to 1.6
- first_norm_bias: float32 [1024], P('row'), may hold values from -2 to 2
- w_query: bfloat16 [1024, 1024], P('row', 'col'), may hold values from -2 to 2
- w_key: bfloat16 [1024, 1024], P('row', 'col'), may hold values from -2 to 2
- w_value: bfloat16 [1024, 1024], P('row', 'col'), may hold values from -0.1875 to 0.1875
- b_query: float32 [1024], P('col'), may hold values from -2 to 2
- b_value: float32 [1024], P('col'), may hold values from -2 to 2
- w_out: bfloat16 [1024, 1024], P('col', 'row'), may hold values from -1.5 to 1.5
- b_out: float32 [1024], P('row'), may hold values from -2 to 2
- second_norm_gain: float32 [1024], P('row'), may hold values from 0.4 to 1.6
- second_norm_bias: float32 [1024], P('row'), may hold values from -2 to 2
- w_fc: bfloat16 [1024, 4096], P('row', 'col'), may hold values from -0.1875 to 0.1875
- b_fc: float32 [4096], P('col'), may hold values from -2 to 2
- w_proj: bfloat16 [4096, 1024], P('col', 'row'), may hold values from -0.09375 to 0.09375
- b_proj: float32 [1024], P('row'), may hold values from -2 to 2
- d_out: bfloat16 [16384, 1024], P(('dp', 'col'), 'row'), may hold values from -6 to 6
Outputs:
- output: bfloat16 [16384, 1024], P(('dp', 'col'), 'row')
- grad_tokens: float32 [16384, 1024], P(('dp', 'col'), 'row')
- grad_ln1_gain: float32 [1024], P('row')
- grad_ln1_bias: float32 [1024], P('row')
- grad_w_query: float32 [1024, 1024], P('row', 'col')
- grad_w_key: float32 [1024, 1024], P('row', 'col')
- grad_w_value: float32 [1024, 1024], P('row', 'col')
- grad_b_query: float32 [1024], P('col')
- grad_b_value: float32 [1024], P('col')
- grad_w_out: float32 [1024, 1024], P('col', 'row')
- grad_b_out: float32 [1024], P('row')
- grad_ln2_gain: float32 [1024], P('row')
- grad_ln2_bias: float32 [1024], P('row')
- grad_w_fc: float32 [1024, 4096], P('row', 'col')
- grad_b_fc: float32 [4096], P('col')
- grad_w_proj: float32 [4096, 1024], P('col', 'row')
- grad_b_proj: float32 [1024], P('row')
The draws below stay inside these ranges and needn't reach their ends.
All inputs are finite; a program needn't handle non-finite values.
Results may differ from the reference program's by a relative error of at most 0.014.
The reference program's roundings to bfloat16 on the way count: a program that leaves them out, or rounds other values in their place, can miss the bound.
Values may be sent and summed in bfloat16 or wider, within the bound.
No kernel may reach another device: no remote copies, remote signals or barrier semaphores. Data moves between devices by JAX's collectives and lax.ppermute only.
A program may use at most 320 MiB of HBM per device.

```python
import jax
import jax.numpy as jnp
from jax import lax

D = 1024
HEADS = 16
HEAD_DIM = 64
FF = 4096
SEQ_LEN = 1024
SEQ_ROW = 1
TOKENS = 16384
N_ROW = 4


def paired_weights(key):
    base = jax.random.fold_in(key, 7)
    first_draw = jax.random.normal(jax.random.fold_in(base, 1), (D, D), jnp.float32)
    second_draw = jax.random.normal(jax.random.fold_in(base, 2), (D, D), jnp.float32)
    first_draw = jnp.clip(first_draw, -6.0, 6.0) * D ** (-0.5)
    second_draw = jnp.clip(second_draw, -6.0, 6.0) * D ** (-0.5)
    return (first_draw, second_draw)


def draw_w_query(key, part):
    first_draw, second_draw = paired_weights(key)
    return jnp.clip(first_draw, -2.0, 2.0).astype(jnp.bfloat16)


def draw_w_key(key, part):
    first_draw, second_draw = paired_weights(key)
    return jnp.clip(second_draw, -2.0, 2.0).astype(jnp.bfloat16)


def steps_of(rng, shape, pieces, least, top_value):
    factor_of = 1.0
    for position, shards_of in pieces:
        draws = jax.random.uniform(jax.random.fold_in(jax.random.fold_in(rng, 6), position), (shards_of,), jnp.float32, least / len(pieces), top_value / len(pieces))
        factor_of = factor_of * jnp.repeat(jnp.exp(draws), shape[position] // shards_of).reshape((-1,) + (1,) * (len(shape) - 1 - position))
    return factor_of


def gaussian(key, dims, width, bound, shards=(), kind=jnp.bfloat16):
    drawn = width * jax.random.normal(key, dims, jnp.float32)
    if shards:
        drawn = drawn * steps_of(key, dims, shards, -0.22, 0.18)
    return jnp.clip(drawn, -bound, bound).astype(kind)


def setup_inputs(seed: int = 0) -> dict:
    splits = jax.random.split(jax.random.key(seed), 18)
    return {
        "tokens": gaussian(splits[0], (TOKENS, D), 1.0, 6.0, ((0, 8), (1, 4))),
        "first_norm_gain": jnp.clip(1.0 + 0.12 * jax.random.normal(splits[1], (D,), jnp.float32), 0.4, 1.6),
        "first_norm_bias": gaussian(splits[2], (D,), 0.5, 2.0, ((0, 4),), jnp.float32),
        "w_query": draw_w_query(jax.random.fold_in(splits[17], 71), 0),
        "w_key": draw_w_key(jax.random.fold_in(splits[17], 71), 0),
        "w_value": gaussian(splits[5], (D, D), D ** -0.5, 0.1875, ((0, 4), (1, 2))),
        "b_query": gaussian(splits[6], (D,), 0.5, 2.0, ((0, 2),), jnp.float32),
        "b_value": gaussian(splits[7], (D,), 0.5, 2.0, ((0, 2),), jnp.float32),
        "w_out": gaussian(splits[8], (D, D), (max(D // 64, 4)) ** -0.5, 1.5, ((0, 2), (1, 4))),
        "b_out": gaussian(splits[9], (D,), 0.5, 2.0, ((0, 4),), jnp.float32),
        "second_norm_gain": jnp.clip(1.0 + 0.12 * jax.random.normal(splits[10], (D,), jnp.float32), 0.4, 1.6),
        "second_norm_bias": gaussian(splits[11], (D,), 0.5, 2.0, ((0, 4),), jnp.float32),
        "w_fc": gaussian(splits[12], (D, FF), D ** -0.5, 0.1875, ((0, 4), (1, 2))),
        "b_fc": gaussian(splits[13], (FF,), 0.5, 2.0, ((0, 2),), jnp.float32),
        "w_proj": gaussian(splits[14], (FF, D), FF ** -0.5, 0.09375, ((0, 2), (1, 4))),
        "b_proj": gaussian(splits[15], (D,), 0.5, 2.0, ((0, 4),), jnp.float32),
        "d_out": gaussian(splits[16], (TOKENS, D), 1.0, 6.0, ((0, 8), (1, 4))),
    }


@jax.custom_vjp
def low(v):
    return lax.optimization_barrier(v.astype(jnp.bfloat16)).astype(jnp.float32)

@jax.custom_vjp
def low_back(v):
    return v

def low_keep(v):
    return (low(v), None)

def low_pass(kept, grad):
    return (grad,)

def back_keep(v):
    return (v, None)

def back_low(kept, grad):
    return (low(grad),)
low.defvjp(low_keep, low_pass)
low_back.defvjp(back_keep, back_low)
EPSILON = 1e-05
HIGHEST = lax.Precision.HIGHEST

def layer_norm(values, gain_vector, bias_vector):
    row_average = lax.optimization_barrier(jnp.mean(values, axis=-1, keepdims=True))
    centred = values - row_average
    spread = lax.optimization_barrier(jnp.mean(centred * centred, axis=-1, keepdims=True))
    return centred * lax.rsqrt(spread + EPSILON) * gain_vector + bias_vector

def product(left_side, right_side):
    return jnp.dot(left_side, right_side, precision=HIGHEST)

def attend(members):
    queries, keys_in, values_in = members
    length_seq = queries.shape[0]
    heads_q = queries.reshape(length_seq, HEADS, HEAD_DIM)
    heads_k = keys_in.reshape(length_seq, HEADS, HEAD_DIM)
    heads_v = values_in.reshape(length_seq, HEADS, HEAD_DIM)
    scores = low_back(jnp.einsum('qhd,khd->hqk', heads_q, heads_k, precision=HIGHEST) * HEAD_DIM ** (-0.5))
    positions = jnp.arange(length_seq)
    causal = positions[:, None] >= positions[None, :]
    scores = jnp.where(causal[None], scores, -1e+30)
    probs_att = low(jax.nn.softmax(scores, axis=-1))
    mixed_out = jnp.einsum('hqk,khd->qhd', probs_att, heads_v, precision=HIGHEST)
    return mixed_out.reshape(length_seq, HEADS * HEAD_DIM)

def forward(inputs, first_norm_gain, first_norm_bias, w_query, w_key, w_value, b_query, b_value, w_out, b_out, second_norm_gain, second_norm_bias, w_fc, b_fc, w_proj, b_proj):
    first_normed = low(layer_norm(inputs, first_norm_gain, first_norm_bias))
    queries = low_back(low(product(first_normed, w_query) + b_query))
    keys_in = low_back(low(product(first_normed, w_key)))
    values_in = low_back(low(product(first_normed, w_value) + b_value))
    seq_total = inputs.shape[0] // SEQ_LEN
    shaped = (queries.reshape(seq_total, SEQ_LEN, D), keys_in.reshape(seq_total, SEQ_LEN, D), values_in.reshape(seq_total, SEQ_LEN, D))
    mixed_out = lax.map(jax.checkpoint(attend), shaped).reshape(-1, D)
    mixed_out = low_back(low(mixed_out))
    middle_stream = inputs + low_back(product(mixed_out, w_out) + b_out)
    second_normed = low(layer_norm(middle_stream, second_norm_gain, second_norm_bias))
    pre_act = low_back(product(second_normed, w_fc) + b_fc)
    hidden = low(jax.nn.gelu(pre_act, approximate=True))
    return middle_stream + low_back(product(hidden, w_proj) + b_proj)

def reference(tokens, first_norm_gain, first_norm_bias, w_query, w_key, w_value, b_query, b_value, w_out, b_out, second_norm_gain, second_norm_bias, w_fc, b_fc, w_proj, b_proj, d_out):
    parameters = tuple((entry.astype(jnp.float32) for entry in (first_norm_gain, first_norm_bias, w_query, w_key, w_value, b_query, b_value, w_out, b_out, second_norm_gain, second_norm_bias, w_fc, b_fc, w_proj, b_proj)))
    group_rows = SEQ_ROW * N_ROW * SEQ_LEN
    groups = tokens.shape[0] // group_rows
    inputs = tokens.astype(jnp.float32).reshape(groups, group_rows, D)
    cotangents = d_out.astype(jnp.float32).reshape(groups, group_rows, D)

    def group_step(totals, members):
        block_in, block_cot = members
        result, pullback = jax.vjp(forward, block_in, *parameters)
        gradients = pullback(block_cot)
        summed = tuple((first_part + second_part for first_part, second_part in zip(totals, gradients[1:])))
        return (summed, (result, gradients[0]))
    starting = tuple((jnp.zeros_like(entry) for entry in parameters))
    totals, (results, d_inputs) = lax.scan(group_step, starting, (inputs, cotangents))
    grad_ln1_gain, grad_ln1_bias, grad_w_query, grad_w_key, grad_w_value, grad_b_query, grad_b_value, grad_w_out, grad_b_out, grad_ln2_gain, grad_ln2_bias, grad_w_fc, grad_b_fc, grad_w_proj, grad_b_proj = totals
    return (results.reshape(-1, D).astype(jnp.bfloat16), d_inputs.reshape(-1, D), grad_ln1_gain, grad_ln1_bias, grad_w_query, grad_w_key, grad_w_value, grad_b_query, grad_b_value, grad_w_out, grad_b_out, grad_ln2_gain, grad_ln2_bias, grad_w_fc, grad_b_fc, grad_w_proj, grad_b_proj)
```

```python
import functools

import jax
import jax.numpy as jnp
from jax import lax
from jax.experimental import pallas as pl
from jax.experimental.pallas import tpu as pltpu
from jax.sharding import PartitionSpec as P

HEAD_DIM = 64
SEQ_LEN = 1024
EPSILON = 1e-05
BF = jnp.bfloat16
F32 = jnp.float32
CHUNKS = 2
NEG = -1e30


def row_swap(value, k):
    size = lax.axis_size("row")
    return lax.ppermute(value, "row", [(i, i ^ k) for i in range(size)])


def col_swap(value):
    return lax.ppermute(value, "col", [(0, 1), (1, 0)])


def after(value, *others):
    return lax.optimization_barrier((value, *others))[0]


def gather_pieces(shard):
    size = lax.axis_size("row")
    pieces = [shard] + [None] * (size - 1)
    if size == 4:
        half = shard.shape[0] // 2
        pieces[1] = row_swap(shard, 1)
        pieces[2] = row_swap(shard, 2)
        top = row_swap(pieces[1][:half], 2)
        bottom = row_swap(pieces[2][half:], 1)
        pieces[3] = jnp.concatenate([top, bottom], axis=0)
    else:
        for k in range(1, size):
            pieces[k] = row_swap(shard, k)
    return pieces


def scatter_sum(partial):
    size = lax.axis_size("row")
    n, width = partial.shape
    f = width // size
    block = [partial[:, k * f : (k + 1) * f] for k in range(size)]
    if size == 4:
        h = n // 2
        send_a = jnp.concatenate([block[1][:h], block[3][:h]], axis=0).astype(BF)
        send_b = jnp.concatenate([block[2][h:], block[3][h:]], axis=0).astype(BF)
        got_a = row_swap(send_a, 1).astype(F32)
        got_b = row_swap(send_b, 2).astype(F32)
        mine_a = block[0][:h] + got_a[:h]
        pass_a = (block[2][:h] + got_a[h:]).astype(BF)
        mine_b = block[0][h:] + got_b[:h]
        pass_b = (block[1][h:] + got_b[h:]).astype(BF)
        return jnp.concatenate(
            [
                mine_a + row_swap(pass_a, 2).astype(F32),
                mine_b + row_swap(pass_b, 1).astype(F32),
            ],
            axis=0,
        )
    total = block[0]
    for k in range(1, size):
        total = total + row_swap(block[k].astype(BF), k).astype(F32)
    return total


def exchange_pairs(size, a, b):
    half = size // 2
    pairs = []
    for row in range(size):
        t, m = row // half, row % half
        for c in range(2):
            pairs.append((row * 2 + c, (c * half + (m ^ a)) * 2 + (t ^ b)))
    return pairs


def tokens_in(values):
    size = lax.axis_size("row")
    half = size // 2
    row, c = lax.axis_index("row"), lax.axis_index("col")
    t, m = row // half, row % half
    rows = values.shape[0] // size
    got = {}
    for a in range(half):
        for b in range(2):
            index = (m ^ a) * 2 + (t ^ b)
            message = lax.dynamic_slice_in_dim(values, index * rows, rows, 0)
            got[a, b] = lax.ppermute(message, ("row", "col"), exchange_pairs(size, a, b))
    same = (t ^ c) == 0
    pieces = []
    for top in range(2):
        for a in range(half):
            pieces.append(jnp.where(same, got[a, top], got[a, 1 - top]))
    return pieces


def tokens_out(pieces):
    size = lax.axis_size("row")
    half = size // 2
    row, c = lax.axis_index("row"), lax.axis_index("col")
    t, m = row // half, row % half
    same = (t ^ c) == 0
    got = {}
    for a in range(half):
        for b in range(2):
            message = jnp.where(same, pieces[b * half + a], pieces[(1 - b) * half + a])
            pairs = [(j, i) for i, j in exchange_pairs(size, a, b)]
            got[a, b] = lax.ppermute(message, ("row", "col"), pairs)
    bit = 1
    while bit < half:
        on = (m & bit) != 0
        got = {(a, b): jnp.where(on, got[a ^ bit, b], got[a, b]) for a, b in got}
        bit *= 2
    on = t != 0
    got = {(a, b): jnp.where(on, got[a, 1 - b], got[a, b]) for a, b in got}
    return jnp.concatenate([got[a, b] for a in range(half) for b in range(2)], axis=0)


def dot_nt(left, right):
    return lax.dot_general(left, right, (((1,), (1,)), ((), ())), preferred_element_type=F32)


def dot_nn(left, right):
    return lax.dot_general(left, right, (((1,), (0,)), ((), ())), preferred_element_type=F32)


def dot_tn(left, right):
    return lax.dot_general(left, right, (((0,), (0,)), ((), ())), preferred_element_type=F32)


def key_chunks(half_rows, block, j, i):
    chunks = []
    if j:
        chunks.append((0, 0, half_rows, False))
    if i:
        chunks.append((j, 0, i * block, False))
    chunks.append((j, i * block, block, True))
    return chunks


def attention_forward_kernel(block, c_ref, x_ref, out_ref, lse_ref):
    half_rows = x_ref.shape[0] // 2
    c = c_ref[0]
    base = [
        pl.multiple_of(c * half_rows, half_rows),
        pl.multiple_of((1 - c) * half_rows, half_rows),
    ]
    low_lane = lax.broadcasted_iota(jnp.int32, (block, 128), 1) < HEAD_DIM
    causal = lax.broadcasted_iota(jnp.int32, (block, block), 0) >= lax.broadcasted_iota(
        jnp.int32, (block, block), 1
    )
    for j in range(2):
        for i in range(half_rows // block):
            rows = pl.ds(base[j] + i * block, block)
            q = x_ref[rows, 0:128] * BF(HEAD_DIM**-0.5)
            outs, lses = [], []
            for head in range(2):
                qm = jnp.where(low_lane == (head == 0), q, BF(0))
                chunks = key_chunks(half_rows, block, j, i)
                scores = []
                for part, start, count, masked in chunks:
                    k = x_ref[pl.ds(base[part] + start, count), 128:256]
                    s = dot_nt(qm, k)
                    scores.append(jnp.where(causal, s, NEG) if masked else s)
                peak = functools.reduce(
                    jnp.maximum, [jnp.max(s, axis=1, keepdims=True) for s in scores]
                )
                exps = [jnp.exp(s - peak) for s in scores]
                total = sum(jnp.sum(e, axis=1, keepdims=True) for e in exps)
                inverse = 1.0 / total
                acc = None
                for e, (part, start, count, masked) in zip(exps, chunks):
                    v = x_ref[pl.ds(base[part] + start, count), 256:384]
                    term = dot_nn((e * inverse).astype(BF), v)
                    acc = term if acc is None else acc + term
                outs.append(acc)
                lses.append(peak + jnp.log(total))
            out_ref[rows, :] = jnp.where(low_lane, outs[0], outs[1]).astype(BF)
            lse_ref[rows, :] = jnp.where(low_lane, lses[0], lses[1])


def attention_backward_kernel(block, c_ref, x_ref, d_ref, lse_ref, out_ref, dk_ref, dv_ref):
    half_rows = x_ref.shape[0] // 2
    c = c_ref[0]
    base = [
        pl.multiple_of(c * half_rows, half_rows),
        pl.multiple_of((1 - c) * half_rows, half_rows),
    ]
    low_lane = lax.broadcasted_iota(jnp.int32, (block, 128), 1) < HEAD_DIM
    causal = lax.broadcasted_iota(jnp.int32, (block, block), 0) >= lax.broadcasted_iota(
        jnp.int32, (block, block), 1
    )
    dk_ref[...] = jnp.zeros_like(dk_ref)
    dv_ref[...] = jnp.zeros_like(dv_ref)
    scale = HEAD_DIM**-0.5
    for j in range(2):
        for i in range(half_rows // block):
            rows = pl.ds(base[j] + i * block, block)
            q = x_ref[rows, 0:128] * BF(scale)
            d = d_ref[rows, :]
            dq = []
            for head in range(2):
                mine = low_lane == (head == 0)
                qm = jnp.where(mine, q, BF(0))
                dm = jnp.where(mine, d, BF(0))
                lse = lse_ref[rows, head * HEAD_DIM : head * HEAD_DIM + 1]
                chunks = key_chunks(half_rows, block, j, i)
                probs, d_probs = [], []
                row_dot = None
                for part, start, count, masked in chunks:
                    where = pl.ds(base[part] + start, count)
                    s = dot_nt(qm, x_ref[where, 128:256])
                    if masked:
                        s = jnp.where(causal, s, NEG)
                    p = jnp.exp(s - lse)
                    dp = dot_nt(dm, x_ref[where, 256:384])
                    term = jnp.sum(p * dp, axis=1, keepdims=True)
                    row_dot = term if row_dot is None else row_dot + term
                    probs.append(p)
                    d_probs.append(dp)
                acc = None
                for p, dp, (part, start, count, masked) in zip(probs, d_probs, chunks):
                    where = pl.ds(base[part] + start, count)
                    ds = (p * (dp - row_dot)).astype(BF)
                    dv_ref[where, :] += dot_tn(p.astype(BF), dm)
                    dk_ref[where, :] += dot_tn(ds, qm)
                    term = dot_nn(ds, x_ref[where, 128:256])
                    acc = term if acc is None else acc + term
                dq.append(acc)
            out_ref[rows, 0:128] = (jnp.where(low_lane, dq[0], dq[1]) * scale).astype(BF)
    out_ref[:, 128:256] = dk_ref[...].astype(BF)
    out_ref[:, 256:384] = dv_ref[...].astype(BF)


def attention_forward(c, triple):
    rows, width = triple.shape
    pairs = width // 384
    block = min(256, rows // 2)
    return pl.pallas_call(
        functools.partial(attention_forward_kernel, block),
        grid_spec=pltpu.PrefetchScalarGridSpec(
            num_scalar_prefetch=1,
            grid=(pairs,),
            in_specs=[pl.BlockSpec((rows, 384), lambda p, c: (0, p))],
            out_specs=[
                pl.BlockSpec((rows, 128), lambda p, c: (0, p)),
                pl.BlockSpec((rows, 128), lambda p, c: (0, p)),
            ],
        ),
        out_shape=[
            jax.ShapeDtypeStruct((rows, pairs * 128), BF),
            jax.ShapeDtypeStruct((rows, pairs * 128), F32),
        ],
        compiler_params=pltpu.CompilerParams(vmem_limit_bytes=48 << 20),
        cost_estimate=pl.CostEstimate(
            flops=pairs * 2 * 4 * rows * rows * 128,
            bytes_accessed=rows * width * 4,
            transcendentals=pairs * 2 * rows * rows // 2,
        ),
        name="attention_forward",
    )(c, triple)


def attention_backward(c, triple, d_mixed, lse):
    rows, width = triple.shape
    pairs = width // 384
    block = min(256, rows // 2)
    return pl.pallas_call(
        functools.partial(attention_backward_kernel, block),
        grid_spec=pltpu.PrefetchScalarGridSpec(
            num_scalar_prefetch=1,
            grid=(pairs,),
            in_specs=[
                pl.BlockSpec((rows, 384), lambda p, c: (0, p)),
                pl.BlockSpec((rows, 128), lambda p, c: (0, p)),
                pl.BlockSpec((rows, 128), lambda p, c: (0, p)),
            ],
            out_specs=pl.BlockSpec((rows, 384), lambda p, c: (0, p)),
            scratch_shapes=[pltpu.VMEM((rows, 128), F32), pltpu.VMEM((rows, 128), F32)],
        ),
        out_shape=jax.ShapeDtypeStruct((rows, width), BF),
        compiler_params=pltpu.CompilerParams(vmem_limit_bytes=48 << 20),
        cost_estimate=pl.CostEstimate(
            flops=pairs * 2 * 10 * rows * rows * 128,
            bytes_accessed=rows * width * 6,
            transcendentals=pairs * 2 * rows * rows // 2,
        ),
        name="attention_backward",
    )(c, triple, d_mixed, lse)


GELU_A = 0.7978845608028654
GELU_B = 0.044715


def mlp_kernel(size, tile, first, *refs):
    refs = list(refs)
    x_ref, d_ref, bias_ref = refs[:3]
    fc_refs = refs[3 : 3 + size]
    proj_refs = refs[3 + size : 3 + 2 * size]
    rest = refs[3 + 2 * size :]
    if not first:
        y_in, dx_in = rest[:2]
        rest = rest[2:]
    y_ref, dx_ref, gp_ref, gf_ref, gb_ref, fc_s, proj_s, hid_s, dpre_s = rest
    rows, width = x_ref.shape
    f = width // size
    for k in range(size):
        fc_s[k * f : (k + 1) * f, :] = fc_refs[k][...]
        proj_s[:, k * f : (k + 1) * f] = proj_refs[k][...]

    @pl.when(pl.program_id(0) == 0)
    def _():
        if first:
            y_ref[...] = jnp.zeros_like(y_ref)
            dx_ref[...] = jnp.zeros_like(dx_ref)
        else:
            y_ref[...] = y_in[...]
            dx_ref[...] = dx_in[...]

    gb_ref[...] = jnp.zeros_like(gb_ref)

    def rows_step(n, carry):
        where = pl.ds(pl.multiple_of(n * tile, tile), tile)
        pre = dot_nn(x_ref[where, :], fc_s[...]) + bias_ref[...]
        dh = dot_nt(d_ref[where, :], proj_s[...])
        square = pre * pre
        th = jnp.tanh(GELU_A * (pre + GELU_B * (square * pre)))
        hid = (0.5 * pre * (1.0 + th)).astype(BF)
        slope = 0.5 * (1.0 + th) + 0.5 * pre * (1.0 - th * th) * (
            GELU_A * (1.0 + (3.0 * GELU_B) * square)
        )
        dpre = (dh * slope).astype(BF)
        hid_s[where, :] = hid
        dpre_s[where, :] = dpre
        gb_ref[...] += jnp.sum(dpre.astype(F32), axis=0, keepdims=True)
        y_ref[where, :] += dot_nn(hid, proj_s[...])
        dx_ref[where, :] += dot_nt(dpre, fc_s[...])
        return carry

    lax.fori_loop(0, rows // tile, rows_step, 0)
    gp_ref[...] = dot_tn(hid_s[...], d_ref[...])
    gf_ref[...] = dot_tn(dpre_s[...], x_ref[...])


def mlp_chunk(x, d, bias, fc, proj, carry):
    rows, width = x.shape
    size = len(fc)
    f = width // size
    hidden = bias.shape[1]
    hb = min(256, hidden)
    first = carry is None
    whole = pl.BlockSpec((rows, width), lambda j: (0, 0), pipeline_mode=pl.Buffered(1))
    in_specs = [whole, whole, pl.BlockSpec((1, hb), lambda j: (0, j))]
    in_specs += [pl.BlockSpec((f, hb), lambda j: (0, j))] * size
    in_specs += [pl.BlockSpec((hb, f), lambda j: (j, 0))] * size
    operands = [x, d, bias, *fc, *proj]
    aliases = {}
    if not first:
        in_specs += [whole, whole]
        aliases = {len(operands): 0, len(operands) + 1: 1}
        operands += list(carry)
    y, dx, gp, gf, gb = pl.pallas_call(
        functools.partial(mlp_kernel, size, min(512, rows), first),
        grid=(hidden // hb,),
        in_specs=in_specs,
        out_specs=[
            whole,
            whole,
            pl.BlockSpec((hb, width), lambda j: (j, 0)),
            pl.BlockSpec((hb, width), lambda j: (j, 0)),
            pl.BlockSpec((1, hb), lambda j: (0, j)),
        ],
        out_shape=[
            jax.ShapeDtypeStruct((rows, width), F32),
            jax.ShapeDtypeStruct((rows, width), F32),
            jax.ShapeDtypeStruct((hidden, width), F32),
            jax.ShapeDtypeStruct((hidden, width), F32),
            jax.ShapeDtypeStruct((1, hidden), F32),
        ],
        scratch_shapes=[
            pltpu.VMEM((width, hb), BF),
            pltpu.VMEM((hb, width), BF),
            pltpu.VMEM((rows, hb), BF),
            pltpu.VMEM((rows, hb), BF),
        ],
        input_output_aliases=aliases,
        compiler_params=pltpu.CompilerParams(vmem_limit_bytes=60 << 20),
        cost_estimate=pl.CostEstimate(
            flops=12 * rows * width * hidden,
            bytes_accessed=rows * width * 20 + hidden * width * 12,
            transcendentals=rows * hidden,
        ),
        name="mlp",
    )(*operands)
    return (y, dx), gp, gf, gb


def norm_stats(values):
    mean = jnp.mean(values, axis=1, keepdims=True)
    centred = values - mean
    inverse = lax.rsqrt(jnp.mean(centred * centred, axis=1, keepdims=True) + EPSILON)
    return centred * inverse, inverse


def norm_backward(gradient, xhat, inverse, gain):
    e = gradient * gain
    back = inverse * (
        e
        - jnp.mean(e, axis=1, keepdims=True)
        - xhat * jnp.mean(e * xhat, axis=1, keepdims=True)
    )
    return back, jnp.sum(gradient * xhat, axis=0), jnp.sum(gradient, axis=0)


def both(own):
    return jnp.concatenate([own, col_swap(own)], axis=0)


def col_sum(partial):
    half = partial.shape[0] // 2
    return partial[:half] + col_swap(partial[half:])


def butterfly(value, axis, k):
    size = lax.axis_size(axis)
    return value + lax.ppermute(value, axis, [(i, i ^ k) for i in range(size)])


def small_sums(scattered, kept):
    size = lax.axis_size("row")
    n, width = scattered.shape
    f = width // size
    blocks = {k: scattered[:, k * f : (k + 1) * f] for k in range(size)}
    bit = 1
    while bit < size:
        stay = [k for k in blocks if not k & bit]
        packed = jnp.concatenate([blocks[k ^ bit].reshape(-1) for k in stay] + [kept])
        got = row_swap(packed, bit)
        blocks = {
            k: blocks[k] + got[i * n * f : (i + 1) * n * f].reshape(n, f)
            for i, k in enumerate(stay)
        }
        kept = kept + got[len(stay) * n * f :]
        bit *= 2
    packed = jnp.concatenate([blocks[0].reshape(-1), kept])
    bit = 1
    while bit < lax.axis_size("dp"):
        packed = butterfly(packed, "dp", bit)
        bit *= 2
    mine = packed[: n * f]
    mine = mine + col_swap(mine)
    return mine.reshape(n, f), packed[n * f :]


def dp_sum(value):
    return lax.psum(value.astype(BF), "dp").astype(F32)


def per_device(
    tokens,
    first_norm_gain,
    first_norm_bias,
    w_query,
    w_key,
    w_value,
    b_query,
    b_value,
    w_out,
    b_out,
    second_norm_gain,
    second_norm_bias,
    w_fc,
    b_fc,
    w_proj,
    b_proj,
    d_out,
):
    col = lax.axis_index("col").astype(jnp.int32).reshape(1)
    f, width = w_query.shape
    size = lax.axis_size("row")
    d_model = f * size
    pairs = width // 128
    hidden = w_fc.shape[1]

    x_own = jnp.concatenate(tokens_in(tokens), axis=1).astype(F32)
    vectors = jnp.stack(
        [first_norm_gain, first_norm_bias, second_norm_gain, second_norm_bias, b_out, b_proj]
    )
    vectors = jnp.concatenate(
        [vectors] + [row_swap(vectors, k) for k in range(1, size)], axis=1
    )
    gain_one, bias_one, gain_two, bias_two, bias_out, bias_proj = vectors
    triple_shard = jnp.stack(
        [w.reshape(f, pairs, 128) for w in (w_query, w_key, w_value)], axis=2
    ).reshape(f, 3 * width)
    w_triple = jnp.concatenate(gather_pieces(triple_shard), axis=0)
    zeros = jnp.zeros((pairs, 128), F32)
    b_triple = jnp.stack(
        [b_query.reshape(pairs, 128), zeros, b_value.reshape(pairs, 128)], axis=1
    ).reshape(1, 3 * width)
    w_out_full = jnp.concatenate(gather_pieces(w_out), axis=1)

    xhat_one, inverse_one = norm_stats(x_own)
    normed_one = both((xhat_one * gain_one + bias_one).astype(BF))
    triple = (dot_nn(normed_one, w_triple) + b_triple).astype(BF)
    mixed, lse = attention_forward(col, triple)
    half = mixed.shape[0] // 2
    sent = col_swap(dot_nn(mixed[half:], w_out_full))
    middle = x_own + (dot_nn(mixed[:half], w_out_full) + sent) + bias_out

    xhat_two, inverse_two = norm_stats(middle)
    normed_two = both((xhat_two * gain_two + bias_two).astype(BF))
    d_own = jnp.concatenate(tokens_in(d_out), axis=1)
    d_full = both(d_own)
    grad_b_proj = jnp.sum(d_own.astype(F32), axis=0)
    carry = None
    hc = hidden // CHUNKS
    grad_fc, grad_proj, grad_b_fc = [], [], []
    for n in range(CHUNKS):
        fc = gather_pieces(w_fc[:, n * hc : (n + 1) * hc])
        proj = gather_pieces(w_proj[n * hc : (n + 1) * hc])
        carry, gp, gf, gb = mlp_chunk(
            normed_two, d_full, b_fc[n * hc : (n + 1) * hc].reshape(1, hc), fc, proj, carry
        )
        grad_proj.append(dp_sum(scatter_sum(gp)))
        grad_fc.append(dp_sum(scatter_sum(gf)).T)
        grad_b_fc.append(gb[0])
    grad_w_proj = jnp.concatenate(grad_proj, axis=0)
    grad_w_fc = jnp.concatenate(grad_fc, axis=1)
    grad_b_fc = jnp.concatenate(grad_b_fc)
    y, d_normed_two = carry
    output = (middle + col_sum(y) + bias_proj).astype(BF)
    output = tokens_out([output[:, k * f : (k + 1) * f] for k in range(size)])

    back_two, grad_gain_two, grad_bias_two = norm_backward(
        col_sum(d_normed_two), xhat_two, inverse_two, gain_two
    )
    d_middle = d_own.astype(F32) + back_two
    d_low = d_middle.astype(BF)
    grad_b_out = jnp.sum(d_low.astype(F32), axis=0)
    d_low_full = both(d_low)
    grad_w_out = dp_sum(scatter_sum(dot_tn(mixed, d_low_full)))
    d_mixed = dot_nt(d_low_full, w_out_full).astype(BF)

    d_triple = attention_backward(col, triple, d_mixed, lse)
    grad_triple = dp_sum(scatter_sum(dot_tn(d_triple, normed_one)))
    grad_triple = grad_triple.reshape(pairs, 3, 128, f)
    grad_query, grad_key, grad_value = (
        grad_triple[:, i].reshape(width, f).T for i in range(3)
    )
    b_sums = jnp.sum(d_triple.astype(F32), axis=0).reshape(pairs, 3, 128)
    d_normed_one = col_sum(dot_nt(d_triple, w_triple))
    back_one, grad_gain_one, grad_bias_one = norm_backward(
        d_normed_one, xhat_one, inverse_one, gain_one
    )
    d_tokens = d_middle + back_one
    grad_tokens = tokens_out([d_tokens[:, k * f : (k + 1) * f] for k in range(size)])

    scattered = jnp.stack(
        [grad_gain_one, grad_bias_one, grad_gain_two, grad_bias_two, grad_b_out, grad_b_proj]
    )
    kept = jnp.concatenate([b_sums[:, 0].reshape(-1), b_sums[:, 2].reshape(-1), grad_b_fc])
    mine, kept = small_sums(scattered, kept)
    return (
        output,
        grad_tokens,
        mine[0],
        mine[1],
        grad_query,
        grad_key,
        grad_value,
        kept[:width],
        kept[width : 2 * width],
        grad_w_out,
        mine[4],
        mine[2],
        mine[3],
        grad_w_fc,
        kept[2 * width :],
        grad_w_proj,
        mine[5],
    )


def solution(mesh):
    token = P(("dp", "col"), "row")
    return jax.shard_map(
        per_device,
        mesh=mesh,
        in_specs=(
            token,
            P("row"),
            P("row"),
            P("row", "col"),
            P("row", "col"),
            P("row", "col"),
            P("col"),
            P("col"),
            P("col", "row"),
            P("row"),
            P("row"),
            P("row"),
            P("row", "col"),
            P("col"),
            P("col", "row"),
            P("row"),
            token,
        ),
        out_specs=(
            token,
            token,
            P("row"),
            P("row"),
            P("row", "col"),
            P("row", "col"),
            P("row", "col"),
            P("col"),
            P("col"),
            P("col", "row"),
            P("row"),
            P("row"),
            P("row"),
            P("row", "col"),
            P("col"),
            P("col", "row"),
            P("row"),
        ),
        check_vma=False,
    )
```
